32 devices in a mesh: dp: 4 (over z), row: 2 (over x), col: 4 (over y, core).
Axes of the slice: x: 2, y: 2, z: 4, core: 2. Of those that a mesh axis runs over, the one named last changes fastest.
Arguments:
- inputs: bfloat16 [4096, 1024], P(('dp', 'col'), 'row'), may hold values from -12 to 12
- qkv_weight: bfloat16 [1024, 3, 1024], P('row', None, 'col'), may hold values from -10 to 10
- qv_bias: float32 [2, 1024], P(None, 'col'), may hold values from -3 to 3
- out_weight: bfloat16 [1024, 1024], P('col', 'row'), may hold values from -1 to 1
- out_bias: float32 [1024], P('row'), may hold values from -3 to 3
- first_gain: float32 [1024], P('row'), may hold values from 0.1 to 1.9
- first_shift: float32 [1024], P('row'), may hold values from -3 to 3
- up_weight: bfloat16 [1024, 4096], P('row', 'col'), may hold values from -0.1875 to 0.1875
- up_bias: float32 [4096], P('col'), may hold values from -3 to 3
- down_weight: bfloat16 [4096, 1024], P('col', 'row'), may hold values from -0.09375 to 0.09375
- down_bias: float32 [1024], P('row'), may hold values from -3 to 3
- second_gain: float32 [1024], P('row'), may hold values from 0.1 to 1.9
- second_shift: float32 [1024], P('row'), may hold values from -3 to 3
- lengths: int32 [8], P(('dp', 'row')), may hold values from 128 to 512, as said below
- out_grad: bfloat16 [4096, 1024], P(('dp', 'col'), 'row'), may hold values from -9 to 9
Outputs:
- block_out: bfloat16 [4096, 1024], P(('dp', 'col'), 'row')
- grad_inputs: float32 [4096, 1024], P(('dp', 'col'), 'row')
- grad_qkv_weight: float32 [1024, 3, 1024], P('row', None, 'col')
- grad_qv_bias: float32 [2, 1024], P(None, 'col')
- grad_out_weight: float32 [1024, 1024], P('col', 'row')
- grad_out_bias: float32 [1024], P('row')
- grad_first_gain: float32 [1024], P('row')
- grad_first_shift: float32 [1024], P('row')
- grad_up_weight: float32 [1024, 4096], P('row', 'col')
- grad_up_bias: float32 [4096], P('col')
- grad_down_weight: float32 [4096, 1024], P('col', 'row')
- grad_down_bias: float32 [1024], P('row')
- grad_second_gain: float32 [1024], P('row')
- grad_second_shift: float32 [1024], P('row')
The draws below stay inside these ranges and needn't reach their ends.
Inputs may be any that keep to these rules, and one draw needn't show every extreme that they name: `lengths`: positions at or past a sequence's length are padding.
All inputs are finite; a program needn't handle non-finite values.
Results may differ from the reference program's by a relative error of at most 0.013.
The reference program's roundings to bfloat16 on the way count: a program that leaves them out, or rounds other values in their place, can miss the bound.
Values may be sent and summed in bfloat16 or wider, within the bound.
A program may use at most 128 MiB of HBM per device.

```python
import math
import jax
import jax.numpy as jnp
from jax import lax

MODEL_WIDTH = 1024
FF = 4096
HEADS = 16
HEAD_DIM = 64
L = 512
SEQS = 8
TOKENS = 4096


def draw_inputs(key, part):
    key_main, key_scale = jax.random.split(key, 2)
    column = jnp.arange(MODEL_WIDTH).astype(jnp.float32)
    rising = 0.4 * jnp.exp(math.log(3.0) * column / (MODEL_WIDTH - 1))
    spread = jnp.exp(jax.random.uniform(key_scale, (MODEL_WIDTH,), jnp.float32, -0.7, 0.7))
    random_part = jnp.clip(jax.random.normal(key_main, (TOKENS, MODEL_WIDTH), jnp.float32), -5.0, 5.0)
    return jnp.clip(random_part * rising * spread, -12.0, 12.0).astype(jnp.bfloat16)


def draw_qkv_weight(key, part):
    key_main = jax.random.fold_in(key, 0)
    drawn = jnp.clip(jax.random.normal(key_main, (MODEL_WIDTH, 3, MODEL_WIDTH), jnp.float32), -6.0, 6.0) * (1.5 / math.sqrt(MODEL_WIDTH))
    return jnp.clip(drawn, -10.0, 10.0).astype(jnp.bfloat16)


def draw_out_grad(key, part):
    key_main = jax.random.fold_in(key, 0)
    row_index = jnp.arange(TOKENS).astype(jnp.float32)
    rising = 0.6 * jnp.exp(math.log(3.0) * row_index / max(TOKENS - 1, 1))
    random_part = jnp.clip(jax.random.normal(key_main, (TOKENS, MODEL_WIDTH), jnp.float32), -5.0, 5.0)
    return jnp.clip(random_part * rising[:, None], -9.0, 9.0).astype(jnp.bfloat16)


def draw_lengths(key, part):
    key_main, key_long, key_short = jax.random.split(key, 3)
    drawn = jax.random.randint(key_main, (SEQS,), L // 4, L + 1)
    longest = jax.random.randint(key_long, (), 0, SEQS)
    shortest = (longest + jax.random.randint(key_short, (), 1, SEQS)) % SEQS
    drawn = drawn.at[longest].set(L).at[shortest].set(L // 4)
    return drawn.astype(jnp.int32)


def steps_of(key, extent, pieces, low, largest):
    def one(axis_at, shards_of):
        draws = jax.random.uniform(jax.random.fold_in(jax.random.fold_in(key, 6), axis_at), (shards_of,), jnp.float32, low / len(pieces), largest / len(pieces))
        return jnp.repeat(jnp.exp(draws), extent[axis_at] // shards_of).reshape((-1,) + (1,) * (len(extent) - axis_at - 1))

    level = one(*pieces[0])
    for cut in pieces[1:]:
        level = level * one(*cut)
    return level


def normal_values(key, shape, width, most, shards=(), kind=jnp.bfloat16):
    array = jax.random.normal(key, shape, jnp.float32) * width
    if len(shards) > 0:
        array = steps_of(key, shape, shards, -0.22, 0.18) * array
    return jnp.clip(array, min=-most, max=most).astype(kind)


def setup_inputs(seed: int = 0) -> dict:
    keys = jax.random.split(jax.random.key(seed), 16)
    inputs = draw_inputs(jax.random.fold_in(keys[15], 71), 0)
    qkv_weight = draw_qkv_weight(jax.random.fold_in(keys[15], 71), 0)
    qv_bias = normal_values(keys[2], (2, MODEL_WIDTH), 0.5, 3.0, ((1, 4),), jnp.float32)
    out_weight = normal_values(keys[3], (MODEL_WIDTH, MODEL_WIDTH), (MODEL_WIDTH * 16 // L) ** -0.5, 1.0, ((0, 4), (1, 2)))
    out_bias = normal_values(keys[4], (MODEL_WIDTH,), 0.5, 3.0, ((0, 2),), jnp.float32)
    first_gain = jnp.clip(1.0 + 0.18 * jax.random.normal(keys[5], (MODEL_WIDTH,), jnp.float32), 0.1, 1.9)
    first_shift = normal_values(keys[6], (MODEL_WIDTH,), 0.5, 3.0, ((0, 2),), jnp.float32)
    up_weight = normal_values(keys[7], (MODEL_WIDTH, FF), MODEL_WIDTH ** -0.5, 0.1875, ((0, 2), (1, 4)))
    up_bias = normal_values(keys[8], (FF,), 0.5, 3.0, ((0, 4),), jnp.float32)
    down_weight = normal_values(keys[9], (FF, MODEL_WIDTH), FF ** -0.5, 0.09375, ((0, 4), (1, 2)))
    down_bias = normal_values(keys[10], (MODEL_WIDTH,), 0.5, 3.0, ((0, 2),), jnp.float32)
    second_gain = jnp.clip(1.0 + 0.18 * jax.random.normal(keys[11], (MODEL_WIDTH,), jnp.float32), 0.1, 1.9)
    second_shift = normal_values(keys[12], (MODEL_WIDTH,), 0.5, 3.0, ((0, 2),), jnp.float32)
    lengths = draw_lengths(jax.random.fold_in(keys[15], 71), 0)
    out_grad = draw_out_grad(jax.random.fold_in(keys[15], 71), 0)
    return {"inputs": inputs, "qkv_weight": qkv_weight, "qv_bias": qv_bias, "out_weight": out_weight, "out_bias": out_bias, "first_gain": first_gain, "first_shift": first_shift, "up_weight": up_weight, "up_bias": up_bias, "down_weight": down_weight, "down_bias": down_bias, "second_gain": second_gain, "second_shift": second_shift, "lengths": lengths, "out_grad": out_grad}


norm_epsilon = 1e-12
masked_score = -1e+30
root_half = 0.7071067811865476
gauss_height = 0.3989422804014327
highest = lax.Precision.HIGHEST

def widen(array_in):
    return array_in.astype(jnp.float32)

def rounded(array_in):
    return lax.optimization_barrier(array_in.astype(jnp.bfloat16)).astype(jnp.float32)

def gelu_pair(preact):
    lower_mass = 0.5 * (1.0 + lax.erf(preact * root_half))
    return (preact * lower_mass, lower_mass + preact * jnp.exp(-0.5 * preact * preact) * gauss_height)

def norm_forward(hidden, norm_gain, norm_shift):
    center = lax.optimization_barrier(jnp.sum(hidden, axis=-1, keepdims=True)) / MODEL_WIDTH
    square = lax.optimization_barrier(jnp.sum(hidden * hidden, axis=-1, keepdims=True)) / MODEL_WIDTH
    rscale = lax.rsqrt(square - center * center + norm_epsilon)
    normed = (hidden - center) * rscale
    return (normed * norm_gain + norm_shift, normed, rscale)

def norm_back(incoming_gradient, normed, rscale, norm_gain):
    scaled = incoming_gradient * norm_gain
    first_mean = lax.optimization_barrier(jnp.sum(scaled, axis=-1, keepdims=True))
    second_mean = lax.optimization_barrier(jnp.sum(scaled * normed, axis=-1, keepdims=True))
    return rscale * (scaled - first_mean / MODEL_WIDTH - normed * (second_mean / MODEL_WIDTH))

def score_block(queries, keys_low, length):
    scores = jnp.einsum('qhd,khd->hqk', widen(queries), widen(keys_low), precision=highest) * HEAD_DIM ** (-0.5)
    visible = jnp.arange(L)[None, None, :] < length
    return jnp.where(visible, scores, masked_score)

def attend(queries, keys_low, values, length):
    scores = score_block(queries, keys_low, length)
    row_peak = lax.optimization_barrier(jnp.max(scores, axis=-1, keepdims=True))
    logsum = row_peak + jnp.log(lax.optimization_barrier(jnp.sum(jnp.exp(scores - row_peak), axis=-1, keepdims=True)))
    soft_weights = rounded(jnp.exp(scores - logsum))
    attention_output = jnp.einsum('hqk,khd->qhd', soft_weights, widen(values), precision=highest)
    return (attention_output.astype(jnp.bfloat16), logsum)

def attend_back(queries, keys_low, values, logsum, incoming_gradient, length):
    scores = score_block(queries, keys_low, length)
    soft_weights = jnp.exp(scores - logsum)
    grad_weights = jnp.einsum('qhd,khd->hqk', widen(incoming_gradient), widen(values), precision=highest)
    row_inner = lax.optimization_barrier(jnp.sum(soft_weights * grad_weights, axis=-1, keepdims=True))
    score_grad = rounded(soft_weights * (grad_weights - row_inner))
    score_scale = HEAD_DIM ** (-0.5)
    grad_queries = jnp.einsum('hqk,khd->qhd', score_grad, widen(keys_low), precision=highest) * score_scale
    grad_keys = jnp.einsum('hqk,qhd->khd', score_grad, widen(queries), precision=highest) * score_scale
    grad_values = jnp.einsum('hqk,qhd->khd', rounded(soft_weights), widen(incoming_gradient), precision=highest)
    return (grad_queries, grad_keys, grad_values)

def reference(inputs, qkv_weight, qv_bias, out_weight, out_bias, first_gain, first_shift, up_weight, up_bias, down_weight, down_bias, second_gain, second_shift, lengths, out_grad):
    qkv_flat = qkv_weight.reshape(MODEL_WIDTH, 3 * MODEL_WIDTH)
    head_shape = (L, HEADS, HEAD_DIM)

    def sequence_step(running_total, sequence_items):
        token_rows, cotangent, length = sequence_items
        projected = jnp.dot(token_rows, qkv_flat, preferred_element_type=jnp.float32).reshape(L, 3, MODEL_WIDTH)
        queries = (projected[:, 0] + qv_bias[0]).astype(jnp.bfloat16).reshape(head_shape)
        keys_low = projected[:, 1].astype(jnp.bfloat16).reshape(head_shape)
        values = (projected[:, 2] + qv_bias[1]).astype(jnp.bfloat16).reshape(head_shape)
        attention_output, logsum = attend(queries, keys_low, values, length)
        attention_output = attention_output.reshape(L, MODEL_WIDTH)
        first_sum = widen(token_rows) + jnp.dot(attention_output, out_weight, preferred_element_type=jnp.float32) + out_bias
        first_norm, first_standardized, first_scale = norm_forward(first_sum, first_gain, first_shift)
        first_reduced = first_norm.astype(jnp.bfloat16)
        preact = jnp.dot(first_reduced, up_weight, preferred_element_type=jnp.float32) + up_bias
        activated, gelu_slope = gelu_pair(preact)
        activation_reduced = activated.astype(jnp.bfloat16)
        second_sum = first_norm + jnp.dot(activation_reduced, down_weight, preferred_element_type=jnp.float32) + down_bias
        second_norm, second_standardized, second_scale = norm_forward(second_sum, second_gain, second_shift)
        incoming_gradient = widen(cotangent)
        second_norm_gradient = norm_back(incoming_gradient, second_standardized, second_scale, second_gain)
        second_reduced = second_norm_gradient.astype(jnp.bfloat16)
        preactivation_gradient = jnp.dot(second_reduced, down_weight.T, preferred_element_type=jnp.float32) * gelu_slope
        preactivation_reduced = preactivation_gradient.astype(jnp.bfloat16)
        norm_gradient_total = second_norm_gradient + jnp.dot(preactivation_reduced, up_weight.T, preferred_element_type=jnp.float32)
        first_norm_gradient = norm_back(norm_gradient_total, first_standardized, first_scale, first_gain)
        residual_reduced = first_norm_gradient.astype(jnp.bfloat16)
        attended_grad = jnp.dot(residual_reduced, out_weight.T, preferred_element_type=jnp.float32).astype(jnp.bfloat16).reshape(head_shape)
        grad_queries, grad_keys, grad_values = attend_back(queries, keys_low, values, logsum, attended_grad, length)
        query_rows_flattened = grad_queries.reshape(L, MODEL_WIDTH)
        value_rows_flattened = grad_values.reshape(L, MODEL_WIDTH)
        combined_heads = jnp.stack([query_rows_flattened, grad_keys.reshape(L, MODEL_WIDTH), value_rows_flattened], axis=1).astype(jnp.bfloat16).reshape(L, 3 * MODEL_WIDTH)
        grad_in = first_norm_gradient + jnp.dot(combined_heads, qkv_flat.T, preferred_element_type=jnp.float32)
        summand_terms = (jnp.dot(token_rows.T, combined_heads, preferred_element_type=jnp.float32).reshape(MODEL_WIDTH, 3, MODEL_WIDTH), jnp.stack([lax.optimization_barrier(jnp.sum(query_rows_flattened, axis=0)), lax.optimization_barrier(jnp.sum(value_rows_flattened, axis=0))]), jnp.dot(attention_output.T, residual_reduced, preferred_element_type=jnp.float32), lax.optimization_barrier(jnp.sum(first_norm_gradient, axis=0)), lax.optimization_barrier(jnp.sum(norm_gradient_total * first_standardized, axis=0)), lax.optimization_barrier(jnp.sum(norm_gradient_total, axis=0)), jnp.dot(first_reduced.T, preactivation_reduced, preferred_element_type=jnp.float32), lax.optimization_barrier(jnp.sum(preactivation_gradient, axis=0)), jnp.dot(activation_reduced.T, second_reduced, preferred_element_type=jnp.float32), lax.optimization_barrier(jnp.sum(second_norm_gradient, axis=0)), lax.optimization_barrier(jnp.sum(incoming_gradient * second_standardized, axis=0)), lax.optimization_barrier(jnp.sum(incoming_gradient, axis=0)))
        running_total = jax.tree.map(jnp.add, running_total, summand_terms)
        return (running_total, (second_norm.astype(jnp.bfloat16), grad_in))
    starting = (jnp.zeros((MODEL_WIDTH, 3, MODEL_WIDTH), jnp.float32), jnp.zeros((2, MODEL_WIDTH), jnp.float32), jnp.zeros((MODEL_WIDTH, MODEL_WIDTH), jnp.float32), jnp.zeros((MODEL_WIDTH,), jnp.float32), jnp.zeros((MODEL_WIDTH,), jnp.float32), jnp.zeros((MODEL_WIDTH,), jnp.float32), jnp.zeros((MODEL_WIDTH, FF), jnp.float32), jnp.zeros((FF,), jnp.float32), jnp.zeros((FF, MODEL_WIDTH), jnp.float32), jnp.zeros((MODEL_WIDTH,), jnp.float32), jnp.zeros((MODEL_WIDTH,), jnp.float32), jnp.zeros((MODEL_WIDTH,), jnp.float32))
    totals, stacked = lax.scan(sequence_step, starting, (inputs.reshape(SEQS, L, MODEL_WIDTH), out_grad.reshape(SEQS, L, MODEL_WIDTH), lengths))
    block_out = stacked[0].reshape(TOKENS, MODEL_WIDTH)
    grad_inputs = stacked[1].reshape(TOKENS, MODEL_WIDTH)
    return (block_out, grad_inputs, totals[0], totals[1], totals[2], totals[3], totals[4], totals[5], totals[6], totals[7], totals[8], totals[9], totals[10], totals[11])
```

```python
import jax
import jax.numpy as jnp
from jax import lax
from jax.experimental import pallas as pl
from jax.experimental.pallas import tpu as pltpu
from jax.sharding import PartitionSpec as P

MODEL_WIDTH = 1024
HEADS = 16
HEAD_DIM = 64
L = 512


norm_epsilon = 1e-12
masked_score = -1e30
root_half = 0.7071067811865476
gauss_height = 0.3989422804014327


def chip_steps(rows, cols):
    steps = [(dr, dc) for dr in range(rows) for dc in range(0, cols, 2)]
    return steps[::-1]


def greet(peers):
    barrier = pltpu.get_barrier_semaphore()
    for peer in peers:
        pl.semaphore_signal(barrier, inc=1, device_id=peer)
    pl.semaphore_wait(barrier, len(peers))


def place(row, col):
    return {"row": row, "col": col}


def send(source, target, send_sem, recv_sem, peer):
    return pltpu.make_async_remote_copy(
        src_ref=source, dst_ref=target, send_sem=send_sem, recv_sem=recv_sem, device_id=peer
    )


def block_of(ref, tiled, rows, cols, row, col):
    if tiled:
        high, wide = ref.shape[0] // cols, ref.shape[1] // rows
        return ref.at[
            pl.ds(pl.multiple_of(col * high, high), high),
            pl.ds(pl.multiple_of(row * wide, wide), wide),
        ]
    high = ref.shape[0] // (rows * cols)
    return ref.at[pl.ds(pl.multiple_of((col * rows + row) * high, high), high), :]


def gather_kernel(tiled, x_ref, out_ref, far_send, far_recv, near_send, near_recv):
    rows, cols = lax.axis_size("row"), lax.axis_size("col")
    r, c = lax.axis_index("row"), lax.axis_index("col")
    mate = c + 1 - 2 * (c % 2)
    steps = chip_steps(rows, cols)
    view = lambda row, col: block_of(out_ref, tiled, rows, cols, row, col)
    greet([place((r + dr) % rows, (c + dc) % cols) for dr, dc in steps[:-1]] + [place(r, mate)])
    copies = []
    for i, (dr, dc) in enumerate(steps[:-1]):
        copies.append(
            send(
                x_ref,
                view(r, c),
                far_send.at[i],
                far_recv.at[i],
                place((r + dr) % rows, (c + dc) % cols),
            )
        )
        copies[-1].start()
    last = len(steps) - 1
    near = [send(x_ref, view(r, c), near_send.at[last], near_recv.at[last], place(r, mate))]
    near[0].start()
    view(r, c)[...] = x_ref[...]
    for i in list(range(1, last)) + [0] if last > 0 else []:
        dr, dc = steps[i]
        row, col = (r - dr + rows) % rows, (c - dc + cols) % cols
        pltpu.make_async_remote_copy(
            src_ref=x_ref,
            dst_ref=view(row, col),
            send_sem=far_send.at[i],
            recv_sem=far_recv.at[i],
            device_id=place(r, mate),
        ).wait_recv()
        near.append(
            send(view(row, col), view(row, col), near_send.at[i], near_recv.at[i], place(r, mate))
        )
        near[-1].start()
    for i, (dr, dc) in enumerate(steps):
        row, col = (r - dr + rows) % rows, (mate - dc + cols) % cols
        pltpu.make_async_remote_copy(
            src_ref=x_ref,
            dst_ref=view(row, col),
            send_sem=near_send.at[i],
            recv_sem=near_recv.at[i],
            device_id=place(r, mate),
        ).wait_recv()
    for copy in copies + near:
        copy.wait_send()


def vmem_spec():
    return pl.BlockSpec(memory_space=pltpu.VMEM)


def gather_blocks(block, tiled, key):
    rows, cols = lax.axis_size("row"), lax.axis_size("col")
    count = rows * cols // 2
    shape = (
        (block.shape[0] * cols, block.shape[1] * rows)
        if tiled
        else (block.shape[0] * rows * cols, block.shape[1])
    )
    return pl.pallas_call(
        lambda *refs: gather_kernel(tiled, *refs),
        out_shape=jax.ShapeDtypeStruct(shape, block.dtype),
        in_specs=[vmem_spec()],
        out_specs=vmem_spec(),
        scratch_shapes=[pltpu.SemaphoreType.DMA((count,))] * 4,
        cost_estimate=pl.CostEstimate(flops=0, bytes_accessed=30000000, transcendentals=0),
        compiler_params=pltpu.CompilerParams(collective_id=key, has_side_effects=True),
        name=f"gather_{key}",
    )(block)


def reduce_kernel(
    tiled,
    turned,
    a_ref,
    b_ref,
    out_ref,
    near_out,
    near_in,
    far_out,
    far_in,
    near_send,
    near_recv,
    far_send,
    far_recv,
):
    rows, cols = lax.axis_size("row"), lax.axis_size("col")
    r, c = lax.axis_index("row"), lax.axis_index("col")
    flip = 1 - 2 * (c % 2)
    mate = c + flip
    steps = chip_steps(rows, cols)
    high, wide = out_ref.shape
    last = len(steps) - 1
    greet([place((r + dr) % rows, (c + dc) % cols) for dr, dc in steps[:-1]] + [place(r, mate)])

    def part(row, col):
        if tiled:
            left = a_ref[pl.ds(pl.multiple_of(col * high, high), high), :]
            right = b_ref[pl.ds(pl.multiple_of(row * wide, wide), wide), :]
        else:
            left = a_ref[pl.ds(pl.multiple_of((col * rows + row) * high, high), high), :]
            right = b_ref[...]
        return lax.dot_general(
            left,
            right,
            (((1,), (1 if turned else 0,)), ((), ())),
            preferred_element_type=jnp.float32,
        )

    copies = []
    for i, (dr, dc) in enumerate(steps):
        row, col = (r + dr) % rows, (c + dc) % cols
        near_out[i] = part(row, col + flip).astype(jnp.bfloat16)
        copies.append(
            send(near_out.at[i], near_in.at[i], near_send.at[i], near_recv.at[i], place(r, mate))
        )
        copies[-1].start()
    near = list(copies)
    far = []
    for i, (dr, dc) in enumerate(steps):
        row, col = (r + dr) % rows, (c + dc) % cols
        total = part(row, col)
        near[i].wait_recv()
        total = total + near_in[i].astype(jnp.float32)
        if i < last:
            far_out[i] = total.astype(jnp.bfloat16)
            far.append(
                send(far_out.at[i], far_in.at[i], far_send.at[i], far_recv.at[i], place(row, col))
            )
            far[-1].start()
        else:
            out_ref[...] = total
    for i in list(range(1, last)) + [0] if last > 0 else []:
        far[i].wait_recv()
        out_ref[...] += far_in[i].astype(jnp.float32)
    for copy in near + far:
        copy.wait_send()


def reduce_blocks(a, b, tiled, turned, key):
    rows, cols = lax.axis_size("row"), lax.axis_size("col")
    count = rows * cols // 2
    width = b.shape[0] if turned else b.shape[1]
    shape = (a.shape[0] // cols, width // rows) if tiled else (a.shape[0] // (rows * cols), width)
    slots = lambda n: pltpu.VMEM((n,) + shape, jnp.bfloat16)
    return pl.pallas_call(
        lambda *refs: reduce_kernel(tiled, turned, *refs),
        out_shape=jax.ShapeDtypeStruct(shape, jnp.float32),
        in_specs=[vmem_spec()] * 2,
        out_specs=vmem_spec(),
        scratch_shapes=[slots(count), slots(count), slots(count - 1), slots(count - 1)]
        + [pltpu.SemaphoreType.DMA((count,))] * 4,
        cost_estimate=pl.CostEstimate(
            flops=2 * a.shape[0] * a.shape[1] * width, bytes_accessed=40000000, transcendentals=0
        ),
        compiler_params=pltpu.CompilerParams(collective_id=key, has_side_effects=True),
        name=f"reduce_{key}",
    )(a, b)


def turn_kernel(x_ref, out_ref, send_sem, recv_sem):
    rows, cols = lax.axis_size("row"), lax.axis_size("col")
    r, c = lax.axis_index("row"), lax.axis_index("col")
    high, wide = out_ref.shape[0], x_ref.shape[1]
    steps = [(dr, dc) for dr in range(rows) for dc in range(cols)][1:]

    def source(row, col):
        return x_ref.at[pl.ds(pl.multiple_of((col * rows + row) * high, high), high), :]

    def target(row, col):
        return out_ref.at[:, pl.ds(pl.multiple_of((col * rows + row) * wide, wide), wide)]

    greet([place((r + dr) % rows, (c + dc) % cols) for dr, dc in steps])
    copies = []
    for i, (dr, dc) in enumerate(steps):
        row, col = (r + dr) % rows, (c + dc) % cols
        copies.append(
            send(source(row, col), target(r, c), send_sem.at[i], recv_sem.at[i], place(row, col))
        )
        copies[-1].start()
    target(r, c)[...] = source(r, c)[...]
    for i, (dr, dc) in enumerate(steps):
        row, col = (r - dr + rows) % rows, (c - dc + cols) % cols
        send(
            source(r, c), target(row, col), send_sem.at[i], recv_sem.at[i], place(row, col)
        ).wait_recv()
    for copy in copies:
        copy.wait_send()


def turn_blocks(x, key):
    group = lax.axis_size("row") * lax.axis_size("col")
    return pl.pallas_call(
        turn_kernel,
        out_shape=jax.ShapeDtypeStruct((x.shape[0] // group, x.shape[1] * group), x.dtype),
        in_specs=[vmem_spec()],
        out_specs=vmem_spec(),
        scratch_shapes=[pltpu.SemaphoreType.DMA((group - 1,))] * 2,
        cost_estimate=pl.CostEstimate(flops=0, bytes_accessed=10000000, transcendentals=0),
        compiler_params=pltpu.CompilerParams(collective_id=key, has_side_effects=True),
        name=f"turn_{key}",
    )(x)


def depth_kernel(x_ref, out_ref, send_sem, recv_sem):
    depth = lax.axis_size("dp")
    d = lax.axis_index("dp")
    greet([{"dp": (d + i) % depth} for i in range(1, depth)])
    copies = []
    for i in range(1, depth):
        copies.append(
            send(
                x_ref,
                out_ref.at[d],
                send_sem.at[i - 1],
                recv_sem.at[i - 1],
                {"dp": (d + i) % depth},
            )
        )
        copies[-1].start()
    out_ref[d] = x_ref[...]
    for i in range(1, depth):
        origin = (d - i + depth) % depth
        send(
            x_ref, out_ref.at[origin], send_sem.at[i - 1], recv_sem.at[i - 1], {"dp": origin}
        ).wait_recv()
    for copy in copies:
        copy.wait_send()


def depth_sum(x, key):
    depth = lax.axis_size("dp")
    stacked = pl.pallas_call(
        depth_kernel,
        out_shape=jax.ShapeDtypeStruct((depth,) + x.shape, x.dtype),
        in_specs=[vmem_spec()],
        out_specs=vmem_spec(),
        scratch_shapes=[pltpu.SemaphoreType.DMA((depth - 1,))] * 2,
        cost_estimate=pl.CostEstimate(flops=0, bytes_accessed=10000000, transcendentals=0),
        compiler_params=pltpu.CompilerParams(collective_id=key, has_side_effects=True),
        name=f"depth_{key}",
    )(x)
    return jnp.sum(stacked, axis=0)


def swap(x, split, join):
    if lax.axis_size("row") != 2:
        return lax.all_to_all(x, "row", split, join, tiled=True)
    r = lax.axis_index("row")
    half = x.shape[split] // 2
    kept = lax.dynamic_slice_in_dim(x, r * half, half, split)
    given = lax.dynamic_slice_in_dim(x, (1 - r) * half, half, split)
    taken = lax.ppermute(given, "row", [(0, 1), (1, 0)])
    low = jnp.where(r == 0, kept, taken)
    high = jnp.where(r == 0, taken, kept)
    return jnp.concatenate([low, high], axis=join)


def widen_rows(x, axis):
    if lax.axis_size("row") != 2:
        return lax.all_gather(x, "row", axis=axis, tiled=True)
    r = lax.axis_index("row")
    other = lax.ppermute(x, "row", [(0, 1), (1, 0)])
    return jnp.concatenate([jnp.where(r == 0, x, other), jnp.where(r == 0, other, x)], axis=axis)


def contract_rows(first_side, second_side):
    return lax.dot_general(
        first_side, second_side, (((0,), (0,)), ((), ())), preferred_element_type=jnp.float32
    )


def gelu_pair(preact):
    lower_mass = 0.5 * (1.0 + lax.erf(preact * root_half))
    return (
        preact * lower_mass,
        lower_mass + preact * jnp.exp(-0.5 * preact * preact) * gauss_height,
    )


def norm_forward(hidden, norm_gain, norm_shift):
    center = jnp.sum(hidden, axis=-1, keepdims=True) / MODEL_WIDTH
    square = jnp.sum(hidden * hidden, axis=-1, keepdims=True) / MODEL_WIDTH
    rscale = lax.rsqrt(square - center * center + norm_epsilon)
    normed = (hidden - center) * rscale
    return (normed * norm_gain + norm_shift, normed, rscale)


def norm_back(incoming_gradient, normed, rscale, norm_gain):
    scaled = incoming_gradient * norm_gain
    first_mean = jnp.sum(scaled, axis=-1, keepdims=True)
    second_mean = jnp.sum(scaled * normed, axis=-1, keepdims=True)
    return rscale * (scaled - first_mean / MODEL_WIDTH - normed * (second_mean / MODEL_WIDTH))


def score_block(queries, keys_low, lengths):
    scores = jnp.einsum(
        "sqhd,skhd->shqk", queries, keys_low, preferred_element_type=jnp.float32
    ) * HEAD_DIM ** (-0.5)
    visible = lax.broadcasted_iota(jnp.int32, (1, 1, 1, L), 3) < lengths[:, None, None, None]
    return jnp.where(visible, scores, masked_score)


def attend(queries, keys_low, values, lengths):
    scores = score_block(queries, keys_low, lengths)
    row_peak = jnp.max(scores, axis=3, keepdims=True)
    logsum = row_peak + jnp.log(jnp.sum(jnp.exp(scores - row_peak), axis=3, keepdims=True))
    soft_weights = jnp.exp(scores - logsum).astype(jnp.bfloat16)
    attention_output = jnp.einsum(
        "shqk,skhd->sqhd", soft_weights, values, preferred_element_type=jnp.float32
    )
    return (attention_output.astype(jnp.bfloat16), logsum)


def attend_back(queries, keys_low, values, logsum, incoming_gradient, lengths):
    scores = score_block(queries, keys_low, lengths)
    soft_weights = jnp.exp(scores - logsum)
    grad_weights = jnp.einsum(
        "sqhd,skhd->shqk", incoming_gradient, values, preferred_element_type=jnp.float32
    )
    row_inner = jnp.sum(soft_weights * grad_weights, axis=3, keepdims=True)
    score_grad = (soft_weights * (grad_weights - row_inner)).astype(jnp.bfloat16)
    score_scale = HEAD_DIM ** (-0.5)
    grad_queries = (
        jnp.einsum("shqk,skhd->sqhd", score_grad, keys_low, preferred_element_type=jnp.float32)
        * score_scale
    )
    grad_keys = (
        jnp.einsum("shqk,sqhd->skhd", score_grad, queries, preferred_element_type=jnp.float32)
        * score_scale
    )
    grad_values = jnp.einsum(
        "shqk,sqhd->skhd",
        soft_weights.astype(jnp.bfloat16),
        incoming_gradient,
        preferred_element_type=jnp.float32,
    )
    return (grad_queries, grad_keys, grad_values)


def shards(
    inputs,
    qkv_weight,
    qv_bias,
    out_weight,
    out_bias,
    first_gain,
    first_shift,
    up_weight,
    up_bias,
    down_weight,
    down_bias,
    second_gain,
    second_shift,
    lengths,
    out_grad,
):
    rows, cols = lax.axis_size("row"), lax.axis_size("col")
    r, c = lax.axis_index("row"), lax.axis_index("col")
    group = rows * cols
    g = c * rows + r
    bf16 = jnp.bfloat16

    def part(x, index, count, axis):
        size = x.shape[axis] // count
        return lax.dynamic_slice_in_dim(x, index * size, size, axis)

    qkv_full = swap(qkv_weight, 2, 0)
    lane = qkv_full.shape[2]
    qkv_flat = qkv_full.reshape(qkv_full.shape[0], -1)
    all_lengths = widen_rows(lengths, 0)
    seqs = all_lengths.shape[0]
    head_shape = (seqs, L, HEADS // group, HEAD_DIM)
    gathered_in = gather_blocks(inputs, True, 0)
    tokens = gathered_in.shape[0]
    vectors = widen_rows(
        jnp.stack([out_bias, first_gain, first_shift, down_bias, second_gain, second_shift]), 1
    )
    out_bias, first_gain, first_shift, down_bias, second_gain, second_shift = [
        vectors[i] for i in range(6)
    ]
    out_full = lax.all_gather(
        lax.all_gather(out_weight, "row", axis=1, tiled=True), "col", axis=0, tiled=True
    )
    up_full = swap(up_weight, 1, 0)
    down_full = swap(down_weight, 0, 1)
    incoming_gradient = swap(out_grad, 0, 1).astype(jnp.float32)
    qv_own = part(qv_bias, r, rows, 1)
    up_own = part(up_bias, r, rows, 0)

    projected = jnp.dot(gathered_in, qkv_flat, preferred_element_type=jnp.float32).reshape(
        tokens, 3, lane
    )
    queries = (projected[:, 0] + qv_own[0]).astype(bf16).reshape(head_shape)
    keys_low = projected[:, 1].astype(bf16).reshape(head_shape)
    values = (projected[:, 2] + qv_own[1]).astype(bf16).reshape(head_shape)
    attention_output, logsum = attend(queries, keys_low, values, all_lengths)
    attended = attention_output.reshape(tokens, lane)
    turned_att = turn_blocks(attended, 1)
    first_sum = (
        part(gathered_in, g, group, 0).astype(jnp.float32)
        + jnp.dot(turned_att, out_full, preferred_element_type=jnp.float32)
        + out_bias
    )
    first_norm, first_standardized, first_scale = norm_forward(first_sum, first_gain, first_shift)
    gathered_norm = gather_blocks(first_norm.astype(bf16), False, 2)
    preact = jnp.dot(gathered_norm, up_full, preferred_element_type=jnp.float32) + up_own
    activated, gelu_slope = gelu_pair(preact)
    activated = activated.astype(bf16)
    second_sum = first_norm + reduce_blocks(activated, down_full, False, False, 3) + down_bias
    second_norm, second_standardized, second_scale = norm_forward(
        second_sum, second_gain, second_shift
    )
    block_out = swap(second_norm.astype(bf16), 1, 0)
    second_norm_gradient = norm_back(
        incoming_gradient, second_standardized, second_scale, second_gain
    )
    gathered_grad = gather_blocks(second_norm_gradient.astype(bf16), False, 4)
    grad_down = swap(contract_rows(activated, gathered_grad).astype(bf16), 1, 0)
    grad_down = lax.psum(grad_down, "dp")
    preactivation_gradient = (
        lax.dot_general(
            gathered_grad,
            down_full,
            (((1,), (1,)), ((), ())),
            preferred_element_type=jnp.float32,
        )
        * gelu_slope
    )
    pre_low = preactivation_gradient.astype(bf16)
    grad_up = swap(contract_rows(gathered_norm, pre_low).astype(bf16), 0, 1)
    norm_gradient_total = second_norm_gradient + reduce_blocks(pre_low, up_full, False, True, 5)
    grad_up, grad_down = lax.optimization_barrier((grad_up, grad_down))
    grad_up = lax.psum(grad_up, "dp")
    first_norm_gradient = norm_back(
        norm_gradient_total, first_standardized, first_scale, first_gain
    )
    gathered_first = gather_blocks(first_norm_gradient.astype(bf16), False, 6)
    grad_out = swap(contract_rows(attended, gathered_first).astype(bf16), 1, 0)
    attended_grad = (
        lax.dot_general(
            gathered_first,
            part(out_full, g, group, 0),
            (((1,), (1,)), ((), ())),
            preferred_element_type=jnp.float32,
        )
        .astype(bf16)
        .reshape(head_shape)
    )
    grad_queries, grad_keys, grad_values = attend_back(
        queries, keys_low, values, logsum, attended_grad, all_lengths
    )
    query_rows_flattened = grad_queries.reshape(tokens, -1)
    value_rows_flattened = grad_values.reshape(tokens, -1)
    combined_heads = jnp.concatenate(
        [query_rows_flattened, grad_keys.reshape(tokens, -1), value_rows_flattened], axis=1
    ).astype(bf16)
    grad_qkv = swap(
        contract_rows(gathered_in, combined_heads).astype(bf16).reshape(qkv_full.shape), 0, 2
    )
    grad_qkv, grad_out, grad_up = lax.optimization_barrier((grad_qkv, grad_out, grad_up))
    grad_qkv = lax.psum(grad_qkv, "dp")
    grad_out = lax.psum(grad_out, "dp")
    first_tile = swap(first_norm_gradient, 1, 0)
    grad_inputs = first_tile + reduce_blocks(combined_heads, qkv_flat, True, True, 7)
    column_part = jnp.stack(
        [
            jnp.sum(first_norm_gradient, axis=0),
            jnp.sum(norm_gradient_total * first_standardized, axis=0),
            jnp.sum(norm_gradient_total, axis=0),
            jnp.sum(second_norm_gradient, axis=0),
            jnp.sum(incoming_gradient * second_standardized, axis=0),
            jnp.sum(incoming_gradient, axis=0),
        ]
    )
    hidden_sum = jnp.sum(preactivation_gradient, axis=0)
    query_sum = jnp.sum(query_rows_flattened, axis=0)
    value_sum = jnp.sum(value_rows_flattened, axis=0)
    width = column_part.shape[1]
    loose = jnp.concatenate([hidden_sum, query_sum, value_sum])
    lines = -(-loose.shape[0] // width)
    lines = -(-(6 + lines) // 8) * 8 - 6
    loose = jnp.pad(loose, (0, lines * width - loose.shape[0])).reshape(lines, width)
    spread = gather_blocks(jnp.concatenate([column_part, loose]), False, 8)
    spread = spread.reshape(cols, rows, 6 + lines, width)
    column_all = jnp.sum(spread[:, :, :6], axis=(0, 1))
    loose_all = lax.dynamic_index_in_dim(spread[:, :, 6:], c, 0, keepdims=False)
    loose_all = loose_all.reshape(rows, lines * width)
    units = hidden_sum.shape[0]
    packed = jnp.concatenate(
        [
            part(column_all, r, rows, 1).reshape(-1),
            loose_all[:, :units].reshape(-1),
            loose_all[:, units : units + lane].reshape(-1),
            loose_all[:, units + lane : units + 2 * lane].reshape(-1),
        ]
    )
    size = packed.shape[0]
    packed = jnp.pad(packed, (0, -size % 1024)).reshape(-1, 128)
    packed = depth_sum(packed, 9).reshape(-1)
    half = width // rows
    column_sums = packed[: 6 * half].reshape(6, half)
    hidden_total = packed[6 * half : 6 * half + rows * units]
    qv_total = packed[6 * half + rows * units : size].reshape(2, rows * lane)
    return (
        block_out,
        grad_inputs,
        grad_qkv.astype(jnp.float32),
        qv_total,
        grad_out.astype(jnp.float32),
        column_sums[0],
        column_sums[1],
        column_sums[2],
        grad_up.astype(jnp.float32),
        hidden_total,
        grad_down.astype(jnp.float32),
        column_sums[3],
        column_sums[4],
        column_sums[5],
    )


def solution(mesh):
    in_specs = (
        P(("dp", "col"), "row"),
        P("row", None, "col"),
        P(None, "col"),
        P("col", "row"),
        P("row"),
        P("row"),
        P("row"),
        P("row", "col"),
        P("col"),
        P("col", "row"),
        P("row"),
        P("row"),
        P("row"),
        P(("dp", "row")),
        P(("dp", "col"), "row"),
    )
    out_specs = (
        P(("dp", "col"), "row"),
        P(("dp", "col"), "row"),
        P("row", None, "col"),
        P(None, "col"),
        P("col", "row"),
        P("row"),
        P("row"),
        P("row"),
        P("row", "col"),
        P("col"),
        P("col", "row"),
        P("row"),
        P("row"),
        P("row"),
    )
    return jax.shard_map(shards, mesh=mesh, in_specs=in_specs, out_specs=out_specs, check_vma=False)
```

```python
import jax
import jax.numpy as jnp
from jax import lax
from jax.experimental import pallas as pl
from jax.experimental.pallas import tpu as pltpu
from jax.sharding import PartitionSpec as P

MODEL_WIDTH = 1024
HEADS = 16
HEAD_DIM = 64
L = 512


norm_epsilon = 1e-12
masked_score = -1e30
root_half = 0.7071067811865476
gauss_height = 0.3989422804014327


def chip_steps(rows, cols):
    steps = [(dr, dc) for dr in range(rows) for dc in range(0, cols, 2)]
    return steps[::-1]


def greet(peers):
    barrier = pltpu.get_barrier_semaphore()
    for peer in peers:
        pl.semaphore_signal(barrier, inc=1, device_id=peer)
    pl.semaphore_wait(barrier, len(peers))


def place(row, col):
    return {"row": row, "col": col}


def send(source, target, send_sem, recv_sem, peer):
    return pltpu.make_async_remote_copy(
        src_ref=source, dst_ref=target, send_sem=send_sem, recv_sem=recv_sem, device_id=peer
    )


def block_of(ref, tiled, rows, cols, row, col):
    if tiled:
        high, wide = ref.shape[0] // cols, ref.shape[1] // rows
        return ref.at[
            pl.ds(pl.multiple_of(col * high, high), high),
            pl.ds(pl.multiple_of(row * wide, wide), wide),
        ]
    high = ref.shape[0] // (rows * cols)
    return ref.at[pl.ds(pl.multiple_of((col * rows + row) * high, high), high), :]


def gather_kernel(tiled, x_ref, out_ref, far_send, far_recv, near_send, near_recv):
    rows, cols = lax.axis_size("row"), lax.axis_size("col")
    r, c = lax.axis_index("row"), lax.axis_index("col")
    mate = c + 1 - 2 * (c % 2)
    steps = chip_steps(rows, cols)
    view = lambda row, col: block_of(out_ref, tiled, rows, cols, row, col)
    greet([place((r + dr) % rows, (c + dc) % cols) for dr, dc in steps[:-1]] + [place(r, mate)])
    copies = []
    for i, (dr, dc) in enumerate(steps[:-1]):
        copies.append(
            send(
                x_ref,
                view(r, c),
                far_send.at[i],
                far_recv.at[i],
                place((r + dr) % rows, (c + dc) % cols),
            )
        )
        copies[-1].start()
    last = len(steps) - 1
    near = [send(x_ref, view(r, c), near_send.at[last], near_recv.at[last], place(r, mate))]
    near[0].start()
    view(r, c)[...] = x_ref[...]
    for i in list(range(1, last)) + [0] if last > 0 else []:
        dr, dc = steps[i]
        row, col = (r - dr + rows) % rows, (c - dc + cols) % cols
        pltpu.make_async_remote_copy(
            src_ref=x_ref,
            dst_ref=view(row, col),
            send_sem=far_send.at[i],
            recv_sem=far_recv.at[i],
            device_id=place(r, mate),
        ).wait_recv()
        near.append(
            send(view(row, col), view(row, col), near_send.at[i], near_recv.at[i], place(r, mate))
        )
        near[-1].start()
    for i, (dr, dc) in enumerate(steps):
        row, col = (r - dr + rows) % rows, (mate - dc + cols) % cols
        pltpu.make_async_remote_copy(
            src_ref=x_ref,
            dst_ref=view(row, col),
            send_sem=near_send.at[i],
            recv_sem=near_recv.at[i],
            device_id=place(r, mate),
        ).wait_recv()
    for copy in copies + near:
        copy.wait_send()


def vmem_spec():
    return pl.BlockSpec(memory_space=pltpu.VMEM)


def gather_blocks(block, tiled, key):
    rows, cols = lax.axis_size("row"), lax.axis_size("col")
    count = rows * cols // 2
    shape = (
        (block.shape[0] * cols, block.shape[1] * rows)
        if tiled
        else (block.shape[0] * rows * cols, block.shape[1])
    )
    return pl.pallas_call(
        lambda *refs: gather_kernel(tiled, *refs),
        out_shape=jax.ShapeDtypeStruct(shape, block.dtype),
        in_specs=[vmem_spec()],
        out_specs=vmem_spec(),
        scratch_shapes=[pltpu.SemaphoreType.DMA((count,))] * 4,
        cost_estimate=pl.CostEstimate(flops=0, bytes_accessed=30000000, transcendentals=0),
        compiler_params=pltpu.CompilerParams(collective_id=key, has_side_effects=True),
        name=f"gather_{key}",
    )(block)


def reduce_kernel(
    tiled,
    turned,
    a_ref,
    b_ref,
    out_ref,
    near_out,
    near_in,
    far_out,
    far_in,
    near_send,
    near_recv,
    far_send,
    far_recv,
):
    rows, cols = lax.axis_size("row"), lax.axis_size("col")
    r, c = lax.axis_index("row"), lax.axis_index("col")
    flip = 1 - 2 * (c % 2)
    mate = c + flip
    steps = chip_steps(rows, cols)
    high, wide = out_ref.shape
    last = len(steps) - 1
    greet([place((r + dr) % rows, (c + dc) % cols) for dr, dc in steps[:-1]] + [place(r, mate)])

    def part(row, col):
        if tiled:
            left = a_ref[pl.ds(pl.multiple_of(col * high, high), high), :]
            right = b_ref[pl.ds(pl.multiple_of(row * wide, wide), wide), :]
        else:
            left = a_ref[pl.ds(pl.multiple_of((col * rows + row) * high, high), high), :]
            right = b_ref[...]
        return lax.dot_general(
            left,
            right,
            (((1,), (1 if turned else 0,)), ((), ())),
            preferred_element_type=jnp.float32,
        )

    copies = []
    for i, (dr, dc) in enumerate(steps):
        row, col = (r + dr) % rows, (c + dc) % cols
        near_out[i] = part(row, col + flip).astype(jnp.bfloat16)
        copies.append(
            send(near_out.at[i], near_in.at[i], near_send.at[i], near_recv.at[i], place(r, mate))
        )
        copies[-1].start()
    near = list(copies)
    far = []
    for i, (dr, dc) in enumerate(steps):
        row, col = (r + dr) % rows, (c + dc) % cols
        total = part(row, col)
        near[i].wait_recv()
        total = total + near_in[i].astype(jnp.float32)
        if i < last:
            far_out[i] = total.astype(jnp.bfloat16)
            far.append(
                send(far_out.at[i], far_in.at[i], far_send.at[i], far_recv.at[i], place(row, col))
            )
            far[-1].start()
        else:
            out_ref[...] = total
    for i in list(range(1, last)) + [0] if last > 0 else []:
        far[i].wait_recv()
        out_ref[...] += far_in[i].astype(jnp.float32)
    for copy in near + far:
        copy.wait_send()


def reduce_blocks(a, b, tiled, turned, key):
    rows, cols = lax.axis_size("row"), lax.axis_size("col")
    count = rows * cols // 2
    width = b.shape[0] if turned else b.shape[1]
    shape = (a.shape[0] // cols, width // rows) if tiled else (a.shape[0] // (rows * cols), width)
    slots = lambda n: pltpu.VMEM((n,) + shape, jnp.bfloat16)
    return pl.pallas_call(
        lambda *refs: reduce_kernel(tiled, turned, *refs),
        out_shape=jax.ShapeDtypeStruct(shape, jnp.float32),
        in_specs=[vmem_spec()] * 2,
        out_specs=vmem_spec(),
        scratch_shapes=[slots(count), slots(count), slots(count - 1), slots(count - 1)]
        + [pltpu.SemaphoreType.DMA((count,))] * 4,
        cost_estimate=pl.CostEstimate(
            flops=2 * a.shape[0] * a.shape[1] * width, bytes_accessed=40000000, transcendentals=0
        ),
        compiler_params=pltpu.CompilerParams(collective_id=key, has_side_effects=True),
        name=f"reduce_{key}",
    )(a, b)


def turn_kernel(x_ref, out_ref, send_sem, recv_sem):
    rows, cols = lax.axis_size("row"), lax.axis_size("col")
    r, c = lax.axis_index("row"), lax.axis_index("col")
    high, wide = out_ref.shape[0], x_ref.shape[1]
    steps = [(dr, dc) for dr in range(rows) for dc in range(cols)][1:]

    def source(row, col):
        return x_ref.at[pl.ds(pl.multiple_of((col * rows + row) * high, high), high), :]

    def target(row, col):
        return out_ref.at[:, pl.ds(pl.multiple_of((col * rows + row) * wide, wide), wide)]

    greet([place((r + dr) % rows, (c + dc) % cols) for dr, dc in steps])
    copies = []
    for i, (dr, dc) in enumerate(steps):
        row, col = (r + dr) % rows, (c + dc) % cols
        copies.append(
            send(source(row, col), target(r, c), send_sem.at[i], recv_sem.at[i], place(row, col))
        )
        copies[-1].start()
    target(r, c)[...] = source(r, c)[...]
    for i, (dr, dc) in enumerate(steps):
        row, col = (r - dr + rows) % rows, (c - dc + cols) % cols
        send(
            source(r, c), target(row, col), send_sem.at[i], recv_sem.at[i], place(row, col)
        ).wait_recv()
    for copy in copies:
        copy.wait_send()


def turn_blocks(x, key):
    group = lax.axis_size("row") * lax.axis_size("col")
    return pl.pallas_call(
        turn_kernel,
        out_shape=jax.ShapeDtypeStruct((x.shape[0] // group, x.shape[1] * group), x.dtype),
        in_specs=[vmem_spec()],
        out_specs=vmem_spec(),
        scratch_shapes=[pltpu.SemaphoreType.DMA((group - 1,))] * 2,
        cost_estimate=pl.CostEstimate(flops=0, bytes_accessed=10000000, transcendentals=0),
        compiler_params=pltpu.CompilerParams(collective_id=key, has_side_effects=True),
        name=f"turn_{key}",
    )(x)


def depth_kernel(x_ref, out_ref, send_sem, recv_sem):
    depth = lax.axis_size("dp")
    d = lax.axis_index("dp")
    greet([{"dp": (d + i) % depth} for i in range(1, depth)])
    copies = []
    for i in range(1, depth):
        copies.append(
            send(
                x_ref,
                out_ref.at[d],
                send_sem.at[i - 1],
                recv_sem.at[i - 1],
                {"dp": (d + i) % depth},
            )
        )
        copies[-1].start()
    out_ref[d] = x_ref[...]
    for i in range(1, depth):
        origin = (d - i + depth) % depth
        send(
            x_ref, out_ref.at[origin], send_sem.at[i - 1], recv_sem.at[i - 1], {"dp": origin}
        ).wait_recv()
    for copy in copies:
        copy.wait_send()


def depth_sum(x, key):
    depth = lax.axis_size("dp")
    stacked = pl.pallas_call(
        depth_kernel,
        out_shape=jax.ShapeDtypeStruct((depth,) + x.shape, x.dtype),
        in_specs=[vmem_spec()],
        out_specs=vmem_spec(),
        scratch_shapes=[pltpu.SemaphoreType.DMA((depth - 1,))] * 2,
        cost_estimate=pl.CostEstimate(flops=0, bytes_accessed=10000000, transcendentals=0),
        compiler_params=pltpu.CompilerParams(collective_id=key, has_side_effects=True),
        name=f"depth_{key}",
    )(x)
    return jnp.sum(stacked, axis=0)


def swap(x, split, join):
    if lax.axis_size("row") != 2:
        return lax.all_to_all(x, "row", split, join, tiled=True)
    r = lax.axis_index("row")
    half = x.shape[split] // 2
    kept = lax.dynamic_slice_in_dim(x, r * half, half, split)
    given = lax.dynamic_slice_in_dim(x, (1 - r) * half, half, split)
    taken = lax.ppermute(given, "row", [(0, 1), (1, 0)])
    low = jnp.where(r == 0, kept, taken)
    high = jnp.where(r == 0, taken, kept)
    return jnp.concatenate([low, high], axis=join)


def widen_rows(x, axis):
    if lax.axis_size("row") != 2:
        return lax.all_gather(x, "row", axis=axis, tiled=True)
    r = lax.axis_index("row")
    other = lax.ppermute(x, "row", [(0, 1), (1, 0)])
    return jnp.concatenate([jnp.where(r == 0, x, other), jnp.where(r == 0, other, x)], axis=axis)


def contract_rows(first_side, second_side):
    return lax.dot_general(
        first_side, second_side, (((0,), (0,)), ((), ())), preferred_element_type=jnp.float32
    )


def gelu_pair(preact):
    lower_mass = 0.5 * (1.0 + lax.erf(preact * root_half))
    return (
        preact * lower_mass,
        lower_mass + preact * jnp.exp(-0.5 * preact * preact) * gauss_height,
    )


def norm_forward(hidden, norm_gain, norm_shift):
    center = jnp.sum(hidden, axis=-1, keepdims=True) / MODEL_WIDTH
    square = jnp.sum(hidden * hidden, axis=-1, keepdims=True) / MODEL_WIDTH
    rscale = lax.rsqrt(square - center * center + norm_epsilon)
    normed = (hidden - center) * rscale
    return (normed * norm_gain + norm_shift, normed, rscale)


def norm_back(incoming_gradient, normed, rscale, norm_gain):
    scaled = incoming_gradient * norm_gain
    first_mean = jnp.sum(scaled, axis=-1, keepdims=True)
    second_mean = jnp.sum(scaled * normed, axis=-1, keepdims=True)
    return rscale * (scaled - first_mean / MODEL_WIDTH - normed * (second_mean / MODEL_WIDTH))


def score_block(queries, keys_low, lengths):
    scores = jnp.einsum(
        "sqhd,skhd->shqk", queries, keys_low, preferred_element_type=jnp.float32
    ) * HEAD_DIM ** (-0.5)
    visible = lax.broadcasted_iota(jnp.int32, (1, 1, 1, L), 3) < lengths[:, None, None, None]
    return jnp.where(visible, scores, masked_score)


def attend(queries, keys_low, values, lengths):
    scores = score_block(queries, keys_low, lengths)
    row_peak = jnp.max(scores, axis=3, keepdims=True)
    logsum = row_peak + jnp.log(jnp.sum(jnp.exp(scores - row_peak), axis=3, keepdims=True))
    soft_weights = jnp.exp(scores - logsum).astype(jnp.bfloat16)
    attention_output = jnp.einsum(
        "shqk,skhd->sqhd", soft_weights, values, preferred_element_type=jnp.float32
    )
    return (attention_output.astype(jnp.bfloat16), logsum)


def attend_back(queries, keys_low, values, logsum, incoming_gradient, lengths):
    scores = score_block(queries, keys_low, lengths)
    soft_weights = jnp.exp(scores - logsum)
    grad_weights = jnp.einsum(
        "sqhd,skhd->shqk", incoming_gradient, values, preferred_element_type=jnp.float32
    )
    row_inner = jnp.sum(soft_weights * grad_weights, axis=3, keepdims=True)
    score_grad = (soft_weights * (grad_weights - row_inner)).astype(jnp.bfloat16)
    score_scale = HEAD_DIM ** (-0.5)
    grad_queries = (
        jnp.einsum("shqk,skhd->sqhd", score_grad, keys_low, preferred_element_type=jnp.float32)
        * score_scale
    )
    grad_keys = (
        jnp.einsum("shqk,sqhd->skhd", score_grad, queries, preferred_element_type=jnp.float32)
        * score_scale
    )
    grad_values = jnp.einsum(
        "shqk,sqhd->skhd",
        soft_weights.astype(jnp.bfloat16),
        incoming_gradient,
        preferred_element_type=jnp.float32,
    )
    return (grad_queries, grad_keys, grad_values)


def shards(
    inputs,
    qkv_weight,
    qv_bias,
    out_weight,
    out_bias,
    first_gain,
    first_shift,
    up_weight,
    up_bias,
    down_weight,
    down_bias,
    second_gain,
    second_shift,
    lengths,
    out_grad,
):
    rows, cols = lax.axis_size("row"), lax.axis_size("col")
    r, c = lax.axis_index("row"), lax.axis_index("col")
    group = rows * cols
    g = c * rows + r
    bf16 = jnp.bfloat16

    def part(x, index, count, axis):
        size = x.shape[axis] // count
        return lax.dynamic_slice_in_dim(x, index * size, size, axis)

    qkv_full = swap(qkv_weight, 2, 0)
    lane = qkv_full.shape[2]
    qkv_flat = qkv_full.reshape(qkv_full.shape[0], -1)
    all_lengths = widen_rows(lengths, 0)
    seqs = all_lengths.shape[0]
    head_shape = (seqs, L, HEADS // group, HEAD_DIM)
    gathered_in = gather_blocks(inputs, True, 0)
    tokens = gathered_in.shape[0]
    vectors = widen_rows(
        jnp.stack([out_bias, first_gain, first_shift, down_bias, second_gain, second_shift]), 1
    )
    out_bias, first_gain, first_shift, down_bias, second_gain, second_shift = [
        vectors[i] for i in range(6)
    ]
    out_wide, gathered_in, up_weight, down_weight = lax.optimization_barrier(
        (widen_rows(out_weight, 1), gathered_in, up_weight, down_weight)
    )
    out_full = lax.all_gather(out_wide, "col", axis=0, tiled=True)
    up_full = swap(up_weight, 1, 0)
    down_full = swap(down_weight, 0, 1)
    incoming_gradient = swap(out_grad, 0, 1).astype(jnp.float32)
    qv_own = part(qv_bias, r, rows, 1)
    up_own = part(up_bias, r, rows, 0)

    projected = jnp.dot(gathered_in, qkv_flat, preferred_element_type=jnp.float32).reshape(
        tokens, 3, lane
    )
    queries = (projected[:, 0] + qv_own[0]).astype(bf16).reshape(head_shape)
    keys_low = projected[:, 1].astype(bf16).reshape(head_shape)
    values = (projected[:, 2] + qv_own[1]).astype(bf16).reshape(head_shape)
    attention_output, logsum = attend(queries, keys_low, values, all_lengths)
    attended = attention_output.reshape(tokens, lane)
    turned_att = turn_blocks(attended, 1)
    first_sum = (
        part(gathered_in, g, group, 0).astype(jnp.float32)
        + jnp.dot(turned_att, out_full, preferred_element_type=jnp.float32)
        + out_bias
    )
    first_norm, first_standardized, first_scale = norm_forward(first_sum, first_gain, first_shift)
    gathered_norm = gather_blocks(first_norm.astype(bf16), False, 2)
    preact = jnp.dot(gathered_norm, up_full, preferred_element_type=jnp.float32) + up_own
    activated, gelu_slope = gelu_pair(preact)
    activated = activated.astype(bf16)
    second_sum = first_norm + reduce_blocks(activated, down_full, False, False, 3) + down_bias
    second_norm, second_standardized, second_scale = norm_forward(
        second_sum, second_gain, second_shift
    )
    block_out = swap(second_norm.astype(bf16), 1, 0)
    second_norm_gradient = norm_back(
        incoming_gradient, second_standardized, second_scale, second_gain
    )
    gathered_grad = gather_blocks(second_norm_gradient.astype(bf16), False, 4)
    grad_down = contract_rows(activated, gathered_grad).astype(bf16)
    preactivation_gradient = (
        lax.dot_general(
            gathered_grad,
            down_full,
            (((1,), (1,)), ((), ())),
            preferred_element_type=jnp.float32,
        )
        * gelu_slope
    )
    pre_low = preactivation_gradient.astype(bf16)
    grad_up = contract_rows(gathered_norm, pre_low).astype(bf16)
    pre_low, grad_up, grad_down = lax.optimization_barrier((pre_low, grad_up, grad_down))
    grad_down = lax.psum(grad_down, "dp")
    norm_gradient_total = second_norm_gradient + reduce_blocks(pre_low, up_full, False, True, 5)
    first_norm_gradient = norm_back(
        norm_gradient_total, first_standardized, first_scale, first_gain
    )
    gathered_first = gather_blocks(first_norm_gradient.astype(bf16), False, 6)
    grad_out = contract_rows(attended, gathered_first).astype(bf16)
    attended_grad = (
        lax.dot_general(
            gathered_first,
            part(out_full, g, group, 0),
            (((1,), (1,)), ((), ())),
            preferred_element_type=jnp.float32,
        )
        .astype(bf16)
        .reshape(head_shape)
    )
    attended_grad, grad_up, grad_down = lax.optimization_barrier(
        (attended_grad, grad_up, grad_down)
    )
    grad_up = lax.psum(grad_up, "dp")
    grad_down = swap(grad_down, 1, 0)
    grad_queries, grad_keys, grad_values = attend_back(
        queries, keys_low, values, logsum, attended_grad, all_lengths
    )
    query_rows_flattened = grad_queries.reshape(tokens, -1)
    value_rows_flattened = grad_values.reshape(tokens, -1)
    combined_heads = jnp.concatenate(
        [query_rows_flattened, grad_keys.reshape(tokens, -1), value_rows_flattened], axis=1
    ).astype(bf16)
    grad_qkv = contract_rows(gathered_in, combined_heads).astype(bf16)
    combined_heads, grad_qkv, grad_out = lax.optimization_barrier(
        (combined_heads, grad_qkv, grad_out)
    )
    back_through = reduce_blocks(combined_heads, qkv_flat, True, True, 7)
    back_through, grad_qkv, grad_out, grad_up = lax.optimization_barrier(
        (back_through, grad_qkv, grad_out, grad_up)
    )
    grad_qkv = lax.psum(grad_qkv, "dp")
    grad_out = lax.psum(grad_out, "dp")
    grad_up = swap(grad_up, 0, 1)
    grad_qkv = swap(grad_qkv.reshape(qkv_full.shape), 0, 2)
    grad_out = swap(grad_out, 1, 0)
    grad_inputs = swap(first_norm_gradient, 1, 0) + back_through
    column_part = jnp.stack(
        [
            jnp.sum(first_norm_gradient, axis=0),
            jnp.sum(norm_gradient_total * first_standardized, axis=0),
            jnp.sum(norm_gradient_total, axis=0),
            jnp.sum(second_norm_gradient, axis=0),
            jnp.sum(incoming_gradient * second_standardized, axis=0),
            jnp.sum(incoming_gradient, axis=0),
        ]
    )
    hidden_sum = jnp.sum(preactivation_gradient, axis=0)
    query_sum = jnp.sum(query_rows_flattened, axis=0)
    value_sum = jnp.sum(value_rows_flattened, axis=0)
    width = column_part.shape[1]
    loose = jnp.concatenate([hidden_sum, query_sum, value_sum])
    lines = -(-loose.shape[0] // width)
    lines = -(-(6 + lines) // 8) * 8 - 6
    loose = jnp.pad(loose, (0, lines * width - loose.shape[0])).reshape(lines, width)
    spread = gather_blocks(jnp.concatenate([column_part, loose]), False, 8)
    spread = spread.reshape(cols, rows, 6 + lines, width)
    column_all = jnp.sum(spread[:, :, :6], axis=(0, 1))
    loose_all = lax.dynamic_index_in_dim(spread[:, :, 6:], c, 0, keepdims=False)
    loose_all = loose_all.reshape(rows, lines * width)
    units = hidden_sum.shape[0]
    packed = jnp.concatenate(
        [
            part(column_all, r, rows, 1).reshape(-1),
            loose_all[:, :units].reshape(-1),
            loose_all[:, units : units + lane].reshape(-1),
            loose_all[:, units + lane : units + 2 * lane].reshape(-1),
        ]
    )
    size = packed.shape[0]
    packed = jnp.pad(packed, (0, -size % 1024)).reshape(-1, 128)
    packed = depth_sum(packed, 9).reshape(-1)
    half = width // rows
    column_sums = packed[: 6 * half].reshape(6, half)
    hidden_total = packed[6 * half : 6 * half + rows * units]
    qv_total = packed[6 * half + rows * units : size].reshape(2, rows * lane)
    return (
        block_out,
        grad_inputs,
        grad_qkv.astype(jnp.float32),
        qv_total,
        grad_out.astype(jnp.float32),
        column_sums[0],
        column_sums[1],
        column_sums[2],
        grad_up.astype(jnp.float32),
        hidden_total,
        grad_down.astype(jnp.float32),
        column_sums[3],
        column_sums[4],
        column_sums[5],
    )


def solution(mesh):
    in_specs = (
        P(("dp", "col"), "row"),
        P("row", None, "col"),
        P(None, "col"),
        P("col", "row"),
        P("row"),
        P("row"),
        P("row"),
        P("row", "col"),
        P("col"),
        P("col", "row"),
        P("row"),
        P("row"),
        P("row"),
        P(("dp", "row")),
        P(("dp", "col"), "row"),
    )
    out_specs = (
        P(("dp", "col"), "row"),
        P(("dp", "col"), "row"),
        P("row", None, "col"),
        P(None, "col"),
        P("col", "row"),
        P("row"),
        P("row"),
        P("row"),
        P("row", "col"),
        P("col"),
        P("col", "row"),
        P("row"),
        P("row"),
        P("row"),
    )
    return jax.shard_map(shards, mesh=mesh, in_specs=in_specs, out_specs=out_specs, check_vma=False)
```

```python
import jax
import jax.numpy as jnp
from jax import lax
from jax.experimental import pallas as pl
from jax.experimental.pallas import tpu as pltpu
from jax.sharding import PartitionSpec as P

MODEL_WIDTH = 1024
HEADS = 16
HEAD_DIM = 64
L = 512


norm_epsilon = 1e-12
masked_score = -1e30
root_half = 0.7071067811865476
gauss_height = 0.3989422804014327


def chip_steps(rows, cols):
    steps = [(dr, dc) for dr in range(rows) for dc in range(0, cols, 2)]
    return steps[::-1]


def greet(peers):
    barrier = pltpu.get_barrier_semaphore()
    for peer in peers:
        pl.semaphore_signal(barrier, inc=1, device_id=peer)
    pl.semaphore_wait(barrier, len(peers))


def place(row, col):
    return {"row": row, "col": col}


def send(source, target, send_sem, recv_sem, peer):
    return pltpu.make_async_remote_copy(
        src_ref=source, dst_ref=target, send_sem=send_sem, recv_sem=recv_sem, device_id=peer
    )


def block_of(ref, tiled, rows, cols, row, col):
    if tiled:
        high, wide = ref.shape[0] // cols, ref.shape[1] // rows
        return ref.at[
            pl.ds(pl.multiple_of(col * high, high), high),
            pl.ds(pl.multiple_of(row * wide, wide), wide),
        ]
    high = ref.shape[0] // (rows * cols)
    return ref.at[pl.ds(pl.multiple_of((col * rows + row) * high, high), high), :]


def gather_kernel(tiled, x_ref, out_ref, far_send, far_recv, near_send, near_recv):
    rows, cols = lax.axis_size("row"), lax.axis_size("col")
    r, c = lax.axis_index("row"), lax.axis_index("col")
    mate = c + 1 - 2 * (c % 2)
    steps = chip_steps(rows, cols)
    view = lambda row, col: block_of(out_ref, tiled, rows, cols, row, col)
    greet([place((r + dr) % rows, (c + dc) % cols) for dr, dc in steps[:-1]] + [place(r, mate)])
    copies = []
    for i, (dr, dc) in enumerate(steps[:-1]):
        copies.append(
            send(
                x_ref,
                view(r, c),
                far_send.at[i],
                far_recv.at[i],
                place((r + dr) % rows, (c + dc) % cols),
            )
        )
        copies[-1].start()
    last = len(steps) - 1
    near = [send(x_ref, view(r, c), near_send.at[last], near_recv.at[last], place(r, mate))]
    near[0].start()
    view(r, c)[...] = x_ref[...]
    for i in list(range(1, last)) + [0] if last > 0 else []:
        dr, dc = steps[i]
        row, col = (r - dr + rows) % rows, (c - dc + cols) % cols
        pltpu.make_async_remote_copy(
            src_ref=x_ref,
            dst_ref=view(row, col),
            send_sem=far_send.at[i],
            recv_sem=far_recv.at[i],
            device_id=place(r, mate),
        ).wait_recv()
        near.append(
            send(view(row, col), view(row, col), near_send.at[i], near_recv.at[i], place(r, mate))
        )
        near[-1].start()
    for i, (dr, dc) in enumerate(steps):
        row, col = (r - dr + rows) % rows, (mate - dc + cols) % cols
        pltpu.make_async_remote_copy(
            src_ref=x_ref,
            dst_ref=view(row, col),
            send_sem=near_send.at[i],
            recv_sem=near_recv.at[i],
            device_id=place(r, mate),
        ).wait_recv()
    for copy in copies + near:
        copy.wait_send()


def vmem_spec():
    return pl.BlockSpec(memory_space=pltpu.VMEM)


def gather_blocks(block, tiled, key):
    rows, cols = lax.axis_size("row"), lax.axis_size("col")
    count = rows * cols // 2
    shape = (
        (block.shape[0] * cols, block.shape[1] * rows)
        if tiled
        else (block.shape[0] * rows * cols, block.shape[1])
    )
    return pl.pallas_call(
        lambda *refs: gather_kernel(tiled, *refs),
        out_shape=jax.ShapeDtypeStruct(shape, block.dtype),
        in_specs=[vmem_spec()],
        out_specs=vmem_spec(),
        scratch_shapes=[pltpu.SemaphoreType.DMA((count,))] * 4,
        cost_estimate=pl.CostEstimate(flops=0, bytes_accessed=30000000, transcendentals=0),
        compiler_params=pltpu.CompilerParams(collective_id=key, has_side_effects=True),
        name=f"gather_{key}",
    )(block)


def reduce_kernel(
    tiled,
    turned,
    a_ref,
    b_ref,
    out_ref,
    near_out,
    near_in,
    far_out,
    far_in,
    near_send,
    near_recv,
    far_send,
    far_recv,
):
    rows, cols = lax.axis_size("row"), lax.axis_size("col")
    r, c = lax.axis_index("row"), lax.axis_index("col")
    flip = 1 - 2 * (c % 2)
    mate = c + flip
    steps = chip_steps(rows, cols)
    high, wide = out_ref.shape
    last = len(steps) - 1
    greet([place((r + dr) % rows, (c + dc) % cols) for dr, dc in steps[:-1]] + [place(r, mate)])

    def part(row, col):
        if tiled:
            left = a_ref[pl.ds(pl.multiple_of(col * high, high), high), :]
            right = b_ref[pl.ds(pl.multiple_of(row * wide, wide), wide), :]
        else:
            left = a_ref[pl.ds(pl.multiple_of((col * rows + row) * high, high), high), :]
            right = b_ref[...]
        return lax.dot_general(
            left,
            right,
            (((1,), (1 if turned else 0,)), ((), ())),
            preferred_element_type=jnp.float32,
        )

    copies = []
    for i, (dr, dc) in enumerate(steps):
        row, col = (r + dr) % rows, (c + dc) % cols
        near_out[i] = part(row, col + flip).astype(jnp.bfloat16)
        copies.append(
            send(near_out.at[i], near_in.at[i], near_send.at[i], near_recv.at[i], place(r, mate))
        )
        copies[-1].start()
    near = list(copies)
    far = []
    for i, (dr, dc) in enumerate(steps):
        row, col = (r + dr) % rows, (c + dc) % cols
        total = part(row, col)
        near[i].wait_recv()
        total = total + near_in[i].astype(jnp.float32)
        if i < last:
            far_out[i] = total.astype(jnp.bfloat16)
            far.append(
                send(far_out.at[i], far_in.at[i], far_send.at[i], far_recv.at[i], place(row, col))
            )
            far[-1].start()
        else:
            out_ref[...] = total
    for i in list(range(1, last)) + [0] if last > 0 else []:
        far[i].wait_recv()
        out_ref[...] += far_in[i].astype(jnp.float32)
    for copy in near + far:
        copy.wait_send()


def reduce_blocks(a, b, tiled, turned, key):
    rows, cols = lax.axis_size("row"), lax.axis_size("col")
    count = rows * cols // 2
    width = b.shape[0] if turned else b.shape[1]
    shape = (a.shape[0] // cols, width // rows) if tiled else (a.shape[0] // (rows * cols), width)
    slots = lambda n: pltpu.VMEM((n,) + shape, jnp.bfloat16)
    return pl.pallas_call(
        lambda *refs: reduce_kernel(tiled, turned, *refs),
        out_shape=jax.ShapeDtypeStruct(shape, jnp.float32),
        in_specs=[vmem_spec()] * 2,
        out_specs=vmem_spec(),
        scratch_shapes=[slots(count), slots(count), slots(count - 1), slots(count - 1)]
        + [pltpu.SemaphoreType.DMA((count,))] * 4,
        cost_estimate=pl.CostEstimate(
            flops=2 * a.shape[0] * a.shape[1] * width, bytes_accessed=40000000, transcendentals=0
        ),
        compiler_params=pltpu.CompilerParams(collective_id=key, has_side_effects=True),
        name=f"reduce_{key}",
    )(a, b)


def turn_kernel(x_ref, out_ref, send_sem, recv_sem):
    rows, cols = lax.axis_size("row"), lax.axis_size("col")
    r, c = lax.axis_index("row"), lax.axis_index("col")
    high, wide = out_ref.shape[0], x_ref.shape[1]
    steps = [(dr, dc) for dr in range(rows) for dc in range(cols)][1:]

    def source(row, col):
        return x_ref.at[pl.ds(pl.multiple_of((col * rows + row) * high, high), high), :]

    def target(row, col):
        return out_ref.at[:, pl.ds(pl.multiple_of((col * rows + row) * wide, wide), wide)]

    greet([place((r + dr) % rows, (c + dc) % cols) for dr, dc in steps])
    copies = []
    for i, (dr, dc) in enumerate(steps):
        row, col = (r + dr) % rows, (c + dc) % cols
        copies.append(
            send(source(row, col), target(r, c), send_sem.at[i], recv_sem.at[i], place(row, col))
        )
        copies[-1].start()
    target(r, c)[...] = source(r, c)[...]
    for i, (dr, dc) in enumerate(steps):
        row, col = (r - dr + rows) % rows, (c - dc + cols) % cols
        send(
            source(r, c), target(row, col), send_sem.at[i], recv_sem.at[i], place(row, col)
        ).wait_recv()
    for copy in copies:
        copy.wait_send()


def turn_blocks(x, key):
    group = lax.axis_size("row") * lax.axis_size("col")
    return pl.pallas_call(
        turn_kernel,
        out_shape=jax.ShapeDtypeStruct((x.shape[0] // group, x.shape[1] * group), x.dtype),
        in_specs=[vmem_spec()],
        out_specs=vmem_spec(),
        scratch_shapes=[pltpu.SemaphoreType.DMA((group - 1,))] * 2,
        cost_estimate=pl.CostEstimate(flops=0, bytes_accessed=10000000, transcendentals=0),
        compiler_params=pltpu.CompilerParams(collective_id=key, has_side_effects=True),
        name=f"turn_{key}",
    )(x)


def depth_kernel(x_ref, out_ref, send_sem, recv_sem):
    depth = lax.axis_size("dp")
    d = lax.axis_index("dp")
    greet([{"dp": (d + i) % depth} for i in range(1, depth)])
    copies = []
    for i in range(1, depth):
        copies.append(
            send(
                x_ref,
                out_ref.at[d],
                send_sem.at[i - 1],
                recv_sem.at[i - 1],
                {"dp": (d + i) % depth},
            )
        )
        copies[-1].start()
    out_ref[d] = x_ref[...]
    for i in range(1, depth):
        origin = (d - i + depth) % depth
        send(
            x_ref, out_ref.at[origin], send_sem.at[i - 1], recv_sem.at[i - 1], {"dp": origin}
        ).wait_recv()
    for copy in copies:
        copy.wait_send()


def depth_sum(x, key):
    depth = lax.axis_size("dp")
    stacked = pl.pallas_call(
        depth_kernel,
        out_shape=jax.ShapeDtypeStruct((depth,) + x.shape, x.dtype),
        in_specs=[vmem_spec()],
        out_specs=vmem_spec(),
        scratch_shapes=[pltpu.SemaphoreType.DMA((depth - 1,))] * 2,
        cost_estimate=pl.CostEstimate(flops=0, bytes_accessed=10000000, transcendentals=0),
        compiler_params=pltpu.CompilerParams(collective_id=key, has_side_effects=True),
        name=f"depth_{key}",
    )(x)
    return jnp.sum(stacked, axis=0)


def swap(x, split, join):
    if lax.axis_size("row") != 2:
        return lax.all_to_all(x, "row", split, join, tiled=True)
    r = lax.axis_index("row")
    half = x.shape[split] // 2
    kept = lax.dynamic_slice_in_dim(x, r * half, half, split)
    given = lax.dynamic_slice_in_dim(x, (1 - r) * half, half, split)
    taken = lax.ppermute(given, "row", [(0, 1), (1, 0)])
    low = jnp.where(r == 0, kept, taken)
    high = jnp.where(r == 0, taken, kept)
    return jnp.concatenate([low, high], axis=join)


def widen_rows(x, axis):
    if lax.axis_size("row") != 2:
        return lax.all_gather(x, "row", axis=axis, tiled=True)
    r = lax.axis_index("row")
    other = lax.ppermute(x, "row", [(0, 1), (1, 0)])
    return jnp.concatenate([jnp.where(r == 0, x, other), jnp.where(r == 0, other, x)], axis=axis)


def contract_rows(first_side, second_side):
    return lax.dot_general(
        first_side, second_side, (((0,), (0,)), ((), ())), preferred_element_type=jnp.float32
    )


def gelu_pair(preact):
    lower_mass = 0.5 * (1.0 + lax.erf(preact * root_half))
    return (
        preact * lower_mass,
        lower_mass + preact * jnp.exp(-0.5 * preact * preact) * gauss_height,
    )


def norm_forward(hidden, norm_gain, norm_shift):
    center = jnp.sum(hidden, axis=-1, keepdims=True) / MODEL_WIDTH
    square = jnp.sum(hidden * hidden, axis=-1, keepdims=True) / MODEL_WIDTH
    rscale = lax.rsqrt(square - center * center + norm_epsilon)
    normed = (hidden - center) * rscale
    return (normed * norm_gain + norm_shift, normed, rscale)


def norm_back(incoming_gradient, normed, rscale, norm_gain):
    scaled = incoming_gradient * norm_gain
    first_mean = jnp.sum(scaled, axis=-1, keepdims=True)
    second_mean = jnp.sum(scaled * normed, axis=-1, keepdims=True)
    return rscale * (scaled - first_mean / MODEL_WIDTH - normed * (second_mean / MODEL_WIDTH))


def score_block(queries, keys_low, lengths):
    scores = jnp.einsum(
        "sqhd,skhd->shqk", queries, keys_low, preferred_element_type=jnp.float32
    ) * HEAD_DIM ** (-0.5)
    visible = lax.broadcasted_iota(jnp.int32, (1, 1, 1, L), 3) < lengths[:, None, None, None]
    return jnp.where(visible, scores, masked_score)


def attend(queries, keys_low, values, lengths):
    scores = score_block(queries, keys_low, lengths)
    row_peak = jnp.max(scores, axis=3, keepdims=True)
    logsum = row_peak + jnp.log(jnp.sum(jnp.exp(scores - row_peak), axis=3, keepdims=True))
    soft_weights = jnp.exp(scores - logsum).astype(jnp.bfloat16)
    attention_output = jnp.einsum(
        "shqk,skhd->sqhd", soft_weights, values, preferred_element_type=jnp.float32
    )
    return (attention_output.astype(jnp.bfloat16), logsum)


def attend_back(queries, keys_low, values, logsum, incoming_gradient, lengths):
    scores = score_block(queries, keys_low, lengths)
    soft_weights = jnp.exp(scores - logsum)
    grad_weights = jnp.einsum(
        "sqhd,skhd->shqk", incoming_gradient, values, preferred_element_type=jnp.float32
    )
    row_inner = jnp.sum(soft_weights * grad_weights, axis=3, keepdims=True)
    score_grad = (soft_weights * (grad_weights - row_inner)).astype(jnp.bfloat16)
    score_scale = HEAD_DIM ** (-0.5)
    grad_queries = (
        jnp.einsum("shqk,skhd->sqhd", score_grad, keys_low, preferred_element_type=jnp.float32)
        * score_scale
    )
    grad_keys = (
        jnp.einsum("shqk,sqhd->skhd", score_grad, queries, preferred_element_type=jnp.float32)
        * score_scale
    )
    grad_values = jnp.einsum(
        "shqk,sqhd->skhd",
        soft_weights.astype(jnp.bfloat16),
        incoming_gradient,
        preferred_element_type=jnp.float32,
    )
    return (grad_queries, grad_keys, grad_values)


def shards(
    inputs,
    qkv_weight,
    qv_bias,
    out_weight,
    out_bias,
    first_gain,
    first_shift,
    up_weight,
    up_bias,
    down_weight,
    down_bias,
    second_gain,
    second_shift,
    lengths,
    out_grad,
):
    rows, cols = lax.axis_size("row"), lax.axis_size("col")
    r, c = lax.axis_index("row"), lax.axis_index("col")
    group = rows * cols
    g = c * rows + r
    bf16 = jnp.bfloat16

    def part(x, index, count, axis):
        size = x.shape[axis] // count
        return lax.dynamic_slice_in_dim(x, index * size, size, axis)

    qkv_full = swap(qkv_weight, 2, 0)
    lane = qkv_full.shape[2]
    qkv_flat = qkv_full.reshape(qkv_full.shape[0], -1)
    all_lengths = widen_rows(lengths, 0)
    seqs = all_lengths.shape[0]
    head_shape = (seqs, L, HEADS // group, HEAD_DIM)
    gathered_in = gather_blocks(inputs, True, 0)
    tokens = gathered_in.shape[0]
    vectors = widen_rows(
        jnp.stack([out_bias, first_gain, first_shift, down_bias, second_gain, second_shift]), 1
    )
    out_bias, first_gain, first_shift, down_bias, second_gain, second_shift = [
        vectors[i] for i in range(6)
    ]
    out_wide, gathered_in, up_weight, down_weight = lax.optimization_barrier(
        (widen_rows(out_weight, 1), gathered_in, up_weight, down_weight)
    )
    out_full = lax.all_gather(out_wide, "col", axis=0, tiled=True)
    up_full = swap(up_weight, 1, 0)
    down_full = swap(down_weight, 0, 1)
    incoming_gradient = swap(out_grad, 0, 1).astype(jnp.float32)
    qv_own = part(qv_bias, r, rows, 1)
    up_own = part(up_bias, r, rows, 0)

    projected = jnp.dot(gathered_in, qkv_flat, preferred_element_type=jnp.float32).reshape(
        tokens, 3, lane
    )
    queries = (projected[:, 0] + qv_own[0]).astype(bf16).reshape(head_shape)
    keys_low = projected[:, 1].astype(bf16).reshape(head_shape)
    values = (projected[:, 2] + qv_own[1]).astype(bf16).reshape(head_shape)
    attention_output, logsum = attend(queries, keys_low, values, all_lengths)
    attended = attention_output.reshape(tokens, lane)
    turned_att = turn_blocks(attended, 1)
    first_sum = (
        part(gathered_in, g, group, 0).astype(jnp.float32)
        + jnp.dot(turned_att, out_full, preferred_element_type=jnp.float32)
        + out_bias
    )
    first_norm, first_standardized, first_scale = norm_forward(first_sum, first_gain, first_shift)
    gathered_norm = gather_blocks(first_norm.astype(bf16), False, 2)
    preact = jnp.dot(gathered_norm, up_full, preferred_element_type=jnp.float32) + up_own
    activated, gelu_slope = gelu_pair(preact)
    activated = activated.astype(bf16)
    second_sum = first_norm + reduce_blocks(activated, down_full, False, False, 3) + down_bias
    second_norm, second_standardized, second_scale = norm_forward(
        second_sum, second_gain, second_shift
    )
    block_out = swap(second_norm.astype(bf16), 1, 0)
    second_norm_gradient = norm_back(
        incoming_gradient, second_standardized, second_scale, second_gain
    )
    gathered_grad = gather_blocks(second_norm_gradient.astype(bf16), False, 4)
    grad_down = contract_rows(activated, gathered_grad).astype(bf16)
    gathered_grad, grad_down = lax.optimization_barrier((gathered_grad, grad_down))
    grad_down = lax.psum(grad_down, "dp")
    preactivation_gradient = (
        lax.dot_general(
            gathered_grad,
            down_full,
            (((1,), (1,)), ((), ())),
            preferred_element_type=jnp.float32,
        )
        * gelu_slope
    )
    pre_low = preactivation_gradient.astype(bf16)
    grad_up = contract_rows(gathered_norm, pre_low).astype(bf16)
    pre_low, grad_up = lax.optimization_barrier((pre_low, grad_up))
    norm_gradient_total = second_norm_gradient + reduce_blocks(pre_low, up_full, False, True, 5)
    first_norm_gradient = norm_back(
        norm_gradient_total, first_standardized, first_scale, first_gain
    )
    gathered_first = gather_blocks(first_norm_gradient.astype(bf16), False, 6)
    grad_out = contract_rows(attended, gathered_first).astype(bf16)
    attended_grad = (
        lax.dot_general(
            gathered_first,
            part(out_full, g, group, 0),
            (((1,), (1,)), ((), ())),
            preferred_element_type=jnp.float32,
        )
        .astype(bf16)
        .reshape(head_shape)
    )
    attended_grad, grad_up, grad_down = lax.optimization_barrier(
        (attended_grad, grad_up, grad_down)
    )
    grad_up = lax.psum(grad_up, "dp")
    grad_down = swap(grad_down, 1, 0)
    grad_queries, grad_keys, grad_values = attend_back(
        queries, keys_low, values, logsum, attended_grad, all_lengths
    )
    query_rows_flattened = grad_queries.reshape(tokens, -1)
    value_rows_flattened = grad_values.reshape(tokens, -1)
    combined_heads = jnp.concatenate(
        [query_rows_flattened, grad_keys.reshape(tokens, -1), value_rows_flattened], axis=1
    ).astype(bf16)
    grad_qkv = contract_rows(gathered_in, combined_heads).astype(bf16)
    grad_qkv = swap(grad_qkv.reshape(qkv_full.shape), 0, 2)
    grad_out = swap(grad_out, 1, 0)
    back_through = reduce_blocks(combined_heads, qkv_flat, True, True, 7)
    back_through, grad_qkv, grad_out, grad_up = lax.optimization_barrier(
        (back_through, grad_qkv, grad_out, grad_up)
    )
    grad_qkv = lax.psum(grad_qkv, "dp")
    grad_out = lax.psum(grad_out, "dp")
    grad_up = swap(grad_up, 0, 1)
    grad_inputs = swap(first_norm_gradient, 1, 0) + back_through
    column_part = jnp.stack(
        [
            jnp.sum(first_norm_gradient, axis=0),
            jnp.sum(norm_gradient_total * first_standardized, axis=0),
            jnp.sum(norm_gradient_total, axis=0),
            jnp.sum(second_norm_gradient, axis=0),
            jnp.sum(incoming_gradient * second_standardized, axis=0),
            jnp.sum(incoming_gradient, axis=0),
        ]
    )
    hidden_sum = jnp.sum(preactivation_gradient, axis=0)
    query_sum = jnp.sum(query_rows_flattened, axis=0)
    value_sum = jnp.sum(value_rows_flattened, axis=0)
    width = column_part.shape[1]
    loose = jnp.concatenate([hidden_sum, query_sum, value_sum])
    lines = -(-loose.shape[0] // width)
    lines = -(-(6 + lines) // 8) * 8 - 6
    loose = jnp.pad(loose, (0, lines * width - loose.shape[0])).reshape(lines, width)
    spread = gather_blocks(jnp.concatenate([column_part, loose]), False, 8)
    spread = spread.reshape(cols, rows, 6 + lines, width)
    column_all = jnp.sum(spread[:, :, :6], axis=(0, 1))
    loose_all = lax.dynamic_index_in_dim(spread[:, :, 6:], c, 0, keepdims=False)
    loose_all = loose_all.reshape(rows, lines * width)
    units = hidden_sum.shape[0]
    packed = jnp.concatenate(
        [
            part(column_all, r, rows, 1).reshape(-1),
            loose_all[:, :units].reshape(-1),
            loose_all[:, units : units + lane].reshape(-1),
            loose_all[:, units + lane : units + 2 * lane].reshape(-1),
        ]
    )
    size = packed.shape[0]
    packed = jnp.pad(packed, (0, -size % 1024)).reshape(-1, 128)
    packed = depth_sum(packed, 9).reshape(-1)
    half = width // rows
    column_sums = packed[: 6 * half].reshape(6, half)
    hidden_total = packed[6 * half : 6 * half + rows * units]
    qv_total = packed[6 * half + rows * units : size].reshape(2, rows * lane)
    return (
        block_out,
        grad_inputs,
        grad_qkv.astype(jnp.float32),
        qv_total,
        grad_out.astype(jnp.float32),
        column_sums[0],
        column_sums[1],
        column_sums[2],
        grad_up.astype(jnp.float32),
        hidden_total,
        grad_down.astype(jnp.float32),
        column_sums[3],
        column_sums[4],
        column_sums[5],
    )


def solution(mesh):
    in_specs = (
        P(("dp", "col"), "row"),
        P("row", None, "col"),
        P(None, "col"),
        P("col", "row"),
        P("row"),
        P("row"),
        P("row"),
        P("row", "col"),
        P("col"),
        P("col", "row"),
        P("row"),
        P("row"),
        P("row"),
        P(("dp", "row")),
        P(("dp", "col"), "row"),
    )
    out_specs = (
        P(("dp", "col"), "row"),
        P(("dp", "col"), "row"),
        P("row", None, "col"),
        P(None, "col"),
        P("col", "row"),
        P("row"),
        P("row"),
        P("row"),
        P("row", "col"),
        P("col"),
        P("col", "row"),
        P("row"),
        P("row"),
        P("row"),
    )
    return jax.shard_map(shards, mesh=mesh, in_specs=in_specs, out_specs=out_specs, check_vma=False)
```
